256 devices in a mesh: cfg: 2 (over core), req: 4 (over y), seq: 32 (over z, x).
Axes of the slice: x: 4, y: 4, z: 8, core: 2. Of those that a mesh axis runs over, the one named last changes fastest.
Arguments:
- patches: float32 [16, 1024, 16], P('req', 'seq'), may hold values from -6 to 6
- noise: float32 [16, 1024, 16], P('req', 'seq'), may hold values from -6 to 6
- timesteps: int32 [16], replicated, may hold values from 50 to 950
- labels: int32 [16], replicated, may hold values from 0 to 999
- lengths: int32 [16], replicated, may hold values from 1 to 1024, 12288 in all
- time_w1: bfloat16 [256, 1152], replicated, may hold values from -0.375 to 0.375
- time_w2: bfloat16 [1152, 1152], replicated, may hold values from -0.1875 to 0.1875
- label_table: bfloat16 [1001, 1152], replicated, may hold values from -5 to 5
- patch_w: bfloat16 [16, 1152], replicated, may hold values from -1.5 to 1.5
- mod_w: bfloat16 [1152, 5760], P(None, ('req', 'seq')), may hold values from -0.1875 to 0.1875
- qkv_w: bfloat16 [1152, 3456], P('req')
- out_w: bfloat16 [1152, 1152], P(None, 'req'), may hold values from -0.1875 to 0.1875
- head_w: bfloat16 [1152, 32], replicated, may hold values from -0.1875 to 0.1875
Outputs:
- guided_update: float32 [16, 1024, 16], P('req', 'seq', 'cfg')
- hidden_norms: float32 [2, 16], P('cfg', 'req')
- max_logits: float32 [2, 16, 16], P('cfg', 'req')
The draws below stay inside these ranges and needn't reach their ends.
Inputs may be any that keep to these rules, and one draw needn't show every extreme that they name: The lengths of the 16 requests sum to 12288, and the longest has exactly 1024 tokens.
All inputs are finite; a program needn't handle non-finite values.
Results may differ from the reference program's by a relative error of at most 0.0029.
Values may be sent and summed in bfloat16 or wider, within the bound.
A program may use at most 128 MiB of HBM per device.

```python
import math
import jax
import jax.numpy as jnp
import numpy as np
from jax import lax

D = 1152
HEADS = 16
FREQ = 256
LABELS = 1000
PATCH_IN = 16
OUT_CH = 32
REQS = 16
SEQ = 1024


def draw_qkv_w(key, part):
    weight_key = jax.random.fold_in(key, 11)
    base = jnp.clip(jax.random.normal(weight_key, (D, 3 * D), jnp.float32), -5.0, 5.0) * D ** (-0.5)
    return base.astype(jnp.bfloat16)


def plant(entries, rng, least, largest):
    longest = entries.shape.index(max(entries.shape))
    spots = []
    for shift in (0, 1):
        where = [jax.random.randint(jax.random.fold_in(rng, axis), (), 0, length) for axis, length in enumerate(entries.shape)]
        where[longest] = (where[longest] + shift) % entries.shape[longest]
        spots.append(tuple(where))
    return entries.at[spots[0]].set(least).at[spots[1]].set(largest)


def steps_of(own_key, extent, pieces, smallest, high):
    loudness, own = 1.0, jax.random.fold_in(own_key, 6)
    for axis_at, blocks in pieces:
        heights = jnp.exp(jax.random.uniform(jax.random.fold_in(own, axis_at), (blocks,), jnp.float32, smallest / len(pieces), high / len(pieces)))
        loudness = loudness * jnp.repeat(heights, extent[axis_at] // blocks).reshape([-1 if axis == axis_at else 1 for axis in range(len(extent))])
    return loudness


def length_profile(number_of, total, limit, skew):
    weights = [(1 << 20) // math.isqrt(standing ** skew) + 1 for standing in range(2, number_of + 1)]
    surplus, counts = total - limit - (number_of - 1), [1] * (number_of - 1)
    while surplus > 0:
        movable = [i for i in range(number_of - 1) if counts[i] < limit]
        mass, budget = sum([weights[i] for i in movable]), surplus
        for i in movable:
            addition = min(limit - counts[i], max(1, budget * weights[i] // mass), surplus)
            counts[i] = counts[i] + addition
            surplus = surplus - addition
    return np.array([limit] + counts)


def uneven_parts(own_key, number_of, total, limit, slope):
    if number_of == 2:
        one = jax.random.randint(own_key, (), max(1, total - limit), min(limit, total - 1) + 1)
        return jnp.stack([one, total - one])
    sizes = jnp.asarray(length_profile(number_of, total, limit, slope), jnp.int32)
    twos = (number_of - 1) // 2
    giver, taker = sizes[1:1 + 2 * twos:2], sizes[2:2 + 2 * twos:2]
    margin = jnp.minimum(giver - 1, limit - taker)
    passed = jax.random.randint(jax.random.fold_in(own_key, 1), (twos,), 0, 1 << 20) % (margin + 1)
    sizes = sizes.at[1:1 + 2 * twos:2].set(giver - passed).at[2:2 + 2 * twos:2].set(taker + passed)
    return sizes[jax.random.permutation(jax.random.fold_in(own_key, 2), number_of)]


def bell_draw(own_key, extent, deviation, limit, split=(), kind=jnp.bfloat16):
    drawn = jax.random.normal(own_key, extent, jnp.float32) * deviation
    if len(split) > 0:
        drawn = steps_of(own_key, extent, split, -0.22, 0.18) * drawn
    return jnp.clip(drawn, min=-limit, max=limit).astype(kind)


def setup_inputs(seed: int = 0) -> dict:
    streams_of = jax.random.split(jax.random.key(seed), 14)
    return {
        "patches": bell_draw(streams_of[0], (REQS, SEQ, PATCH_IN), 1.0, 6.0, ((0, 4), (1, 32)), jnp.float32),
        "noise": bell_draw(streams_of[1], (REQS, SEQ, PATCH_IN), 1.0, 6.0, ((0, 4), (1, 32)), jnp.float32),
        "timesteps": plant(jax.random.randint(streams_of[2], (REQS,), 50, 951), jax.random.fold_in(streams_of[2], 1), 50, 950).astype(jnp.int32),
        "labels": plant(jax.random.randint(streams_of[3], (REQS,), 0, LABELS), jax.random.fold_in(streams_of[3], 1), 0, LABELS - 1).astype(jnp.int32),
        "lengths": uneven_parts(streams_of[4], REQS, 3 * REQS * SEQ // 4, SEQ, 2).astype(jnp.int32),
        "time_w1": bell_draw(streams_of[5], (FREQ, D), FREQ ** -0.5, 0.375),
        "time_w2": bell_draw(streams_of[6], (D, D), D ** -0.5, 0.1875),
        "label_table": bell_draw(streams_of[7], (LABELS + 1, D), 1.0, 5.0),
        "patch_w": bell_draw(streams_of[8], (PATCH_IN, D), PATCH_IN ** -0.5, 1.5),
        "mod_w": bell_draw(streams_of[9], (D, 5 * D), D ** -0.5, 0.1875, ((1, 128),)),
        "qkv_w": draw_qkv_w(jax.random.fold_in(streams_of[13], 71), 0),
        "out_w": bell_draw(streams_of[11], (D, D), D ** -0.5, 0.1875, ((1, 4),)),
        "head_w": bell_draw(streams_of[12], (D, OUT_CH), D ** -0.5, 0.1875),
    }


norm_eps = 1e-06
masked_score = -1e+30
guide_scale = 4.0
plan_offset = 0.008
diffusion_steps = 1000.0

def layer_norm(values):
    center = values - lax.optimization_barrier(jnp.mean(values, axis=-1, keepdims=True))
    spread = lax.optimization_barrier(jnp.mean(center * center, axis=-1, keepdims=True))
    return center * lax.rsqrt(spread + norm_eps)

def sine_table(places, count, cos_first):
    half = count // 2
    rates = jnp.exp(-math.log(10000.0) * jnp.arange(half, dtype=jnp.float32) / half)
    angles = places.astype(jnp.float32)[:, None] * rates[None, :]
    if cos_first:
        return jnp.concatenate([jnp.cos(angles), jnp.sin(angles)], axis=1)
    return jnp.concatenate([jnp.sin(angles), jnp.cos(angles)], axis=1)

def alpha_bar(steps):
    phase = (steps / diffusion_steps + plan_offset) / (1.0 + plan_offset) * (math.pi / 2.0)
    return jnp.cos(phase) ** 2

def sampler_step(patches, noise, guided, varpart, steps, valid):
    abar = alpha_bar(steps)
    abar_prev = alpha_bar(steps - 1.0)
    beta = 1.0 - abar / abar_prev
    start = (patches - jnp.sqrt(1.0 - abar) * guided) / jnp.sqrt(abar)
    mean = beta * jnp.sqrt(abar_prev) / (1.0 - abar) * start + (1.0 - abar_prev) * jnp.sqrt(1.0 - beta) / (1.0 - abar) * patches
    tilde = beta * (1.0 - abar_prev) / (1.0 - abar)
    frac = (varpart + 1.0) * 0.5
    logvar = frac * jnp.log(beta) + (1.0 - frac) * jnp.log(tilde)
    return jnp.where(valid, mean + jnp.exp(0.5 * logvar) * noise, 0.0)

def reference(patches, noise, timesteps, labels, lengths, time_w1, time_w2, label_table, patch_w, mod_w, qkv_w, out_w, head_w):
    tfreq = sine_table(timesteps, FREQ, True).astype(jnp.bfloat16)
    time_hidden = jax.nn.silu(jnp.dot(tfreq, time_w1, preferred_element_type=jnp.float32)).astype(jnp.bfloat16)
    time_embed = jnp.dot(time_hidden, time_w2, preferred_element_type=jnp.float32)
    places = jnp.arange(SEQ, dtype=jnp.int32)
    position = sine_table(places, D, False)
    head_dim = D // HEADS

    def one_request(items):
        patch_rows, modulation, length = items
        shift1 = modulation[0:D]
        scale1 = modulation[D:2 * D]
        gate1 = modulation[2 * D:3 * D]
        shift2 = modulation[3 * D:4 * D]
        scale2 = modulation[4 * D:5 * D]
        hidden0 = jnp.dot(patch_rows.astype(jnp.bfloat16), patch_w, preferred_element_type=jnp.float32) + position
        normed1 = (layer_norm(hidden0) * (1.0 + scale1) + shift1).astype(jnp.bfloat16)
        projected = jnp.dot(normed1, qkv_w, preferred_element_type=jnp.float32)
        query = projected[:, :D].astype(jnp.bfloat16).reshape(SEQ, HEADS, head_dim)
        keys = projected[:, D:2 * D].astype(jnp.bfloat16).reshape(SEQ, HEADS, head_dim)
        values = projected[:, 2 * D:].astype(jnp.bfloat16).reshape(SEQ, HEADS, head_dim)
        scores = jnp.einsum('qhd,khd->hqk', query.astype(jnp.float32), keys.astype(jnp.float32)) / math.sqrt(head_dim)
        key_ok = (places < length)[None, None, :]
        scores = jnp.where(key_ok, scores, masked_score)
        row_max = lax.optimization_barrier(jnp.max(scores, axis=2))
        expo = jnp.where(key_ok, jnp.exp(scores - row_max[:, :, None]), 0.0)
        total = lax.optimization_barrier(jnp.sum(expo, axis=2))
        weights = expo.astype(jnp.bfloat16)
        mixed = jnp.einsum('hqk,khd->qhd', weights.astype(jnp.float32), values.astype(jnp.float32)) / jnp.transpose(total)[:, :, None]
        mixed = mixed.astype(jnp.bfloat16).reshape(SEQ, D)
        hidden1 = hidden0 + gate1 * jnp.dot(mixed, out_w, preferred_element_type=jnp.float32)
        query_ok = places < length
        squares = jnp.sum(jnp.where(query_ok[:, None], hidden1 * hidden1, 0.0))
        norm_value = jnp.sqrt(squares / (length.astype(jnp.float32) * D))
        top = lax.optimization_barrier(jnp.max(jnp.where(query_ok[None, :], row_max, masked_score), axis=1))
        normed2 = (layer_norm(hidden1) * (1.0 + scale2) + shift2).astype(jnp.bfloat16)
        prediction = jnp.dot(normed2, head_w, preferred_element_type=jnp.float32)
        return (prediction, norm_value, top)
    results = []
    for copy in range(2):
        if copy == 0:
            label_used = labels
        else:
            label_used = jnp.full_like(labels, LABELS)
        cond = time_embed + label_table[label_used].astype(jnp.float32)
        cond_act = jax.nn.silu(cond).astype(jnp.bfloat16)
        modulation = jnp.dot(cond_act, mod_w, preferred_element_type=jnp.float32)
        results.append(lax.map(one_request, (patches, modulation, lengths)))
    pred_cond, norm_cond, top_cond = results[0]
    pred_uncond, norm_uncond, top_uncond = results[1]
    eps_cond = pred_cond[..., :PATCH_IN]
    eps_uncond = pred_uncond[..., :PATCH_IN]
    guided = eps_uncond + guide_scale * (eps_cond - eps_uncond)
    varpart = pred_cond[..., PATCH_IN:]
    steps = timesteps.astype(jnp.float32)[:, None, None]
    valid = (places[None, :] < lengths[:, None])[:, :, None]
    guided_update = sampler_step(patches, noise, guided, varpart, steps, valid)
    hidden_norms = jnp.stack([norm_cond, norm_uncond], axis=0)
    max_logits = jnp.stack([top_cond, top_uncond], axis=0)
    return (guided_update, hidden_norms, max_logits)
```

```python
import math

import jax
import jax.numpy as jnp
import numpy as np
from jax import lax
from jax.experimental import pallas as pl
from jax.experimental.pallas import tpu as pltpu
from jax.sharding import PartitionSpec as P

HEADS = 16
FREQ = 256
D = 1152
SEQ_TOTAL = 1024
NSEQ = 32
NREQ = 4
NDEV = NSEQ * NREQ
GROUP = 8
SLOT = 32
BLK = 128
WIN = 256
PAIR = 144
HEAD_DIM = 72
ROWS = 288
HALF = 144
MODC = 45
MESH = pl.DeviceIdType.MESH

norm_eps = 1e-06
masked_score = -1e30
guide_scale = 4.0
plan_offset = 0.008
diffusion_steps = 1000.0
INV_ROOT = 1.0 / math.sqrt(HEAD_DIM)
EXP_SCALE = INV_ROOT * math.log2(math.e)


def time_table(places):
    half = FREQ // 2
    rates = jnp.exp(-math.log(10000.0) * jnp.arange(half, dtype=jnp.float32) / half)
    angles = places.astype(jnp.float32)[:, None] * rates[None, :]
    return jnp.concatenate([jnp.cos(angles), jnp.sin(angles)], axis=1)


def position_factors():
    half = D // 2
    rates = np.exp(-math.log(10000.0) * np.arange(half) / half)
    coarse = (SLOT * np.arange(NSEQ))[:, None] * rates[None, :]
    fine = np.arange(SLOT)[:, None] * rates[None, :]
    sc, cc, sf, cf = np.sin(coarse), np.cos(coarse), np.sin(fine), np.cos(fine)
    p1 = np.concatenate([sc, cc], axis=1)[:, None, :]
    p2 = np.concatenate([cc, -sc], axis=1)[:, None, :]
    q1 = np.concatenate([cf, cf], axis=1)
    q2 = np.concatenate([sf, sf], axis=1)
    return [jnp.asarray(t.astype(np.float32)) for t in (p1, p2, q1, q2)]


def alpha_bar(steps):
    phase = (steps / diffusion_steps + plan_offset) / (1.0 + plan_offset) * (math.pi / 2.0)
    return jnp.cos(phase) ** 2


def sampler_step(patches, noise, guided, varpart, steps, valid):
    abar = alpha_bar(steps)
    abar_prev = alpha_bar(steps - 1.0)
    beta = 1.0 - abar / abar_prev
    start = (patches - jnp.sqrt(1.0 - abar) * guided) / jnp.sqrt(abar)
    mean = (
        beta * jnp.sqrt(abar_prev) / (1.0 - abar) * start
        + (1.0 - abar_prev) * jnp.sqrt(1.0 - beta) / (1.0 - abar) * patches
    )
    tilde = beta * (1.0 - abar_prev) / (1.0 - abar)
    frac = (varpart + 1.0) * 0.5
    logvar = frac * jnp.log(beta) + (1.0 - frac) * jnp.log(tilde)
    return jnp.where(valid, mean + jnp.exp(0.5 * logvar) * noise, 0.0)


def layer_norm(values):
    center = values - jnp.mean(values, axis=-1, keepdims=True)
    spread = jnp.mean(center * center, axis=-1, keepdims=True)
    return center * lax.rsqrt(spread + norm_eps)


def kernel(
    len_ref, patches_ref, modp_ref, qkv_hbm, outw_hbm, headw_ref, patchw_ref, p1_ref, p2_ref, q1_ref, q2_ref,
    pred_out, stat_out,
    pb, patch_all, mod_all, mod_rows, wbuf, outbuf, qbuf, kbuf, vbuf, mbuf, mixin, att, predsend, pred_in, stat_send, stat_in, top,
    mod_s, mod_r, pat_s, pat_r, w_s, w_r, wl, wf_s, wf_r, o_s, o_r, ol, of_s, of_r, mx_s, mx_r, pr_s, pr_r, st_s, st_r,
):
    g = lax.axis_index("cfg")
    y = lax.axis_index("req")
    s = lax.axis_index("seq")
    other = 1 - g
    me = y * NSEQ + s
    q = lax.div(s, GROUP)
    j = lax.rem(s, GROUP)

    def remote(src, dst, ssem, rsem, dev):
        return pltpu.make_async_remote_copy(
            src_ref=src, dst_ref=dst, send_sem=ssem, recv_sem=rsem, device_id=dev, device_id_type=MESH
        )

    bar = pltpu.get_barrier_semaphore()

    def greet(k, _):
        d = lax.rem(me + k, NDEV)
        pl.semaphore_signal(bar, inc=1, device_id=(g, lax.div(d, NSEQ), lax.rem(d, NSEQ)), device_id_type=MESH)
        return 0

    lax.fori_loop(1, NDEV, greet, 0)
    for qq in range(NREQ):
        pl.semaphore_signal(bar, inc=1, device_id=(other, y, qq * GROUP + lax.div(s, NREQ)), device_id_type=MESH)
    pl.semaphore_signal(bar, inc=1, device_id=(other, y, s), device_id_type=MESH)

    pb[...] = patches_ref[...].astype(jnp.bfloat16)
    col = pl.multiple_of(j * BLK, BLK)
    local_w = []
    for kind in range(3):
        c = pltpu.make_async_copy(
            qkv_hbm.at[:, pl.ds(pl.multiple_of(kind * D + col, BLK), WIN)],
            wbuf.at[kind, pl.ds(pl.multiple_of(ROWS * y, 16), ROWS), :],
            wl.at[kind],
        )
        c.start()
        local_w.append(c)
    local_o = pltpu.make_async_copy(outw_hbm, outbuf.at[y], ol)
    local_o.start()
    pl.semaphore_wait(bar, NDEV - 1 + NREQ + 1)

    def send_mod(k, _):
        d = lax.rem(me + k, NDEV)
        dy, dq = lax.div(d, NSEQ), lax.rem(d, NSEQ)
        row = dy * NREQ + lax.div(dq, GROUP)
        remote(modp_ref.at[row], mod_all.at[me], mod_s, mod_r, (g, dy, dq)).start()
        return 0

    lax.fori_loop(1, NDEV, send_mod, 0)

    def send_patch(k, _):
        d = lax.rem(s + k, NSEQ)
        remote(pb.at[lax.div(d, GROUP)], patch_all.at[s], pat_s, pat_r, (g, y, d)).start()
        return 0

    lax.fori_loop(1, NSEQ, send_patch, 0)

    w_copies = []
    for dy in range(1, NREQ):
        ty = lax.rem(y + dy, NREQ)
        for kind in range(3):
            c = remote(
                qkv_hbm.at[pl.ds(pl.multiple_of(HALF * g, 16), HALF), pl.ds(pl.multiple_of(kind * D + col, BLK), WIN)],
                wbuf.at[kind, pl.ds(pl.multiple_of(ROWS * y + HALF * g, 16), HALF), :],
                w_s.at[dy - 1, kind],
                w_r.at[dy - 1, kind],
                (g, ty, s),
            )
            c.start()
            w_copies.append((dy, c))

    mod_all[me] = modp_ref[y * NREQ + q]
    patch_all[s] = pb[q]

    w_forwards = []
    for dy in range(1, NREQ):
        for dd, c in w_copies:
            if dd == dy:
                c.wait_recv()
        sy = lax.rem(y + NREQ - dy, NREQ)
        part = wbuf.at[:, pl.ds(pl.multiple_of(ROWS * sy + HALF * g, 16), HALF), :]
        f = remote(part, part, wf_s.at[dy - 1], wf_r.at[dy - 1], (other, y, s))
        f.start()
        w_forwards.append(f)

    pltpu.make_async_copy(mod_all.at[pl.ds(0, NDEV - 1)], mod_all.at[pl.ds(0, NDEV - 1)], mod_r).wait()

    o_copies = []
    for dy in range(1, NREQ):
        ty = lax.rem(y + dy, NREQ)
        rows = pl.ds(pl.multiple_of((D // 2) * g, 16), D // 2)
        c = remote(outw_hbm.at[rows, :], outbuf.at[y, rows, :], o_s.at[dy - 1], o_r.at[dy - 1], (g, ty, s))
        c.start()
        o_copies.append(c)

    lane_row = lax.broadcasted_iota(jnp.int32, (1, BLK), 1)
    for tile in range(5 * D // BLK):
        first = (tile * BLK) // MODC
        last = (tile * BLK + BLK - 1) // MODC
        value = None
        for source in range(first, last + 1):
            at = source * MODC - tile * BLK
            piece = mod_all[source]
            if at % BLK:
                piece = pltpu.roll(piece, at % BLK, 1)
            value = piece if value is None else jnp.where(lane_row >= at, piece, value)
        mod_rows[tile // 9, :, (tile % 9) * BLK : (tile % 9 + 1) * BLK] = value

    length = len_ref[y * NREQ + q]
    pltpu.make_async_copy(patch_all.at[pl.ds(0, NSEQ - 1)], patch_all.at[pl.ds(0, NSEQ - 1)], pat_r).wait()
    for f in w_forwards:
        f.wait_recv()
    for c in local_w:
        c.wait()

    lane = lax.broadcasted_iota(jnp.int32, (1, WIN), 1)
    low = j * 16
    in_a = (lane >= low) & (lane < low + HEAD_DIM)
    in_b = (lane >= low + HEAD_DIM) & (lane < low + PAIR)
    spare = lane == lax.rem(low + PAIR, WIN)

    def embed(first_source, count):
        x = patch_all[pl.ds(first_source, count)].reshape(count * SLOT, 16)
        h = jnp.dot(x, patchw_ref[...], preferred_element_type=jnp.float32)
        places = [
            p1_ref[first_source + i] * q1_ref[...] + p2_ref[first_source + i] * q2_ref[...] for i in range(count)
        ]
        return h + jnp.concatenate(places, axis=0)

    def project(b, _):
        h = embed(b * 8, 8)
        normed = (layer_norm(h) * (1.0 + mod_rows[1]) + mod_rows[0]).astype(jnp.bfloat16)
        rows = pl.ds(pl.multiple_of(b * 256, 256), 256)
        qbuf[rows, :] = jnp.dot(normed, wbuf[0], preferred_element_type=jnp.float32).astype(jnp.bfloat16)
        keys = jnp.dot(normed, wbuf[1], preferred_element_type=jnp.float32)
        place = b * 256 + lax.broadcasted_iota(jnp.int32, (256, 1), 0)
        bias = jnp.where(place < length, 0.0, masked_score)
        kbuf[rows, :] = jnp.where(spare, bias, keys).astype(jnp.bfloat16)
        vbuf[rows, :] = jnp.dot(normed, wbuf[2], preferred_element_type=jnp.float32).astype(jnp.bfloat16)
        return 0

    lax.fori_loop(0, 4, project, 0)

    top[...] = jnp.full_like(top, masked_score)

    def attend(k, _):
        b = lax.rem(j + k, GROUP)
        rows = pl.ds(pl.multiple_of(b * BLK, BLK), BLK)
        query = qbuf[rows, :].astype(jnp.float32)
        live = b * BLK + lax.broadcasted_iota(jnp.int32, (BLK, 1), 0) < length
        mixed = jnp.zeros((BLK, WIN), jnp.float32)
        for head, inside in enumerate((in_a, in_b)):
            mine = jnp.where(inside, query, jnp.where(spare, 1.0, 0.0)).astype(jnp.bfloat16)
            raw = lax.dot_general(mine, kbuf[...], (((1,), (1,)), ((), ())), preferred_element_type=jnp.float32)
            peak = jnp.max(raw, axis=1, keepdims=True)
            expo = jnp.exp2((raw - peak) * EXP_SCALE)
            total = jnp.sum(expo, axis=1, keepdims=True)
            summed = jnp.dot(expo.astype(jnp.bfloat16), vbuf[...], preferred_element_type=jnp.float32)
            mixed = jnp.where(inside, summed * (1.0 / total), mixed)
            best = jnp.max(jnp.where(live, peak, masked_score), axis=0, keepdims=True)
            top[head] = jnp.maximum(top[head], best)
        mbuf[b] = mixed.astype(jnp.bfloat16)

        @pl.when(k < GROUP)
        def _():
            remote(mbuf.at[b], mixin.at[j], mx_s, mx_r, (g, y, q * GROUP + b)).start()

        return 0

    lax.fori_loop(1, GROUP + 1, attend, 0)
    mixin[j] = mbuf[j]

    o_forwards = []
    for dy in range(1, NREQ):
        o_copies[dy - 1].wait_recv()
        sy = lax.rem(y + NREQ - dy, NREQ)
        part = outbuf.at[sy, pl.ds(pl.multiple_of((D // 2) * g, 16), D // 2), :]
        f = remote(part, part, of_s.at[dy - 1], of_r.at[dy - 1], (other, y, s))
        f.start()
        o_forwards.append(f)
    hidden0 = embed(j * 4, 4)
    local_o.wait()
    for f in o_forwards:
        f.wait_recv()
    pltpu.make_async_copy(mixin.at[pl.ds(0, GROUP - 1)], mixin.at[pl.ds(0, GROUP - 1)], mx_r).wait()

    pieces = []
    for part in range(NREQ):
        acc = jnp.zeros((BLK, ROWS), jnp.float32)
        for pair in range(GROUP):
            acc += jnp.dot(
                mixin[pair], outbuf[part, pair * BLK : pair * BLK + WIN, :], preferred_element_type=jnp.float32
            )
        pieces.append(acc)
    attended = jnp.concatenate(pieces, axis=1)
    hidden1 = hidden0 + mod_rows[2] * attended
    place = j * BLK + lax.broadcasted_iota(jnp.int32, (BLK, 1), 0)
    squares = jnp.sum(jnp.sum(jnp.where(place < length, hidden1 * hidden1, 0.0), axis=1, keepdims=True), axis=0, keepdims=True)
    stat = jnp.where(lane_row == 0, squares, jnp.where(lane_row == 1, top[0], top[1]) * INV_ROOT)
    stat_send[...] = stat

    def send_stat(k, _):
        d = lax.rem(s + k, NSEQ)
        remote(stat_send, stat_in.at[s], st_s, st_r, (g, y, d)).start()
        return 0

    lax.fori_loop(1, NSEQ, send_stat, 0)
    stat_in[s] = stat

    normed2 = (layer_norm(hidden1) * (1.0 + mod_rows[4]) + mod_rows[3]).astype(jnp.bfloat16)
    prediction = jnp.dot(normed2, headw_ref[...], preferred_element_type=jnp.float32)
    predsend[...] = prediction.reshape(NREQ, SLOT, 32)
    slot = g * NREQ + q
    p_copies = []
    for i in range(NREQ):
        for gg in range(2):
            ts = j * NREQ + i
            self_copy = (ts == s) & (g == gg)
            c = remote(predsend.at[i], pred_in.at[slot], pr_s.at[i * 2 + gg], pr_r, (gg, y, ts))
            p_copies.append((self_copy, c))

            @pl.when(jnp.logical_not(self_copy))
            def _():
                c.start()

            @pl.when(self_copy)
            def _():
                pltpu.make_async_copy(predsend.at[i], pred_in.at[slot], pr_r).start()

    pltpu.make_async_copy(pred_in, pred_in, pr_r).wait()
    pltpu.make_async_copy(stat_in.at[pl.ds(0, NSEQ - 1)], stat_in.at[pl.ds(0, NSEQ - 1)], st_r).wait()
    pred_out[...] = pred_in[...]
    stat_out[...] = stat_in[...]

    pltpu.make_async_copy(mod_all.at[pl.ds(0, NDEV - 1)], mod_all.at[pl.ds(0, NDEV - 1)], mod_s).wait()
    pltpu.make_async_copy(patch_all.at[pl.ds(0, NSEQ - 1)], patch_all.at[pl.ds(0, NSEQ - 1)], pat_s).wait()
    pltpu.make_async_copy(mixin.at[pl.ds(0, GROUP - 1)], mixin.at[pl.ds(0, GROUP - 1)], mx_s).wait()
    pltpu.make_async_copy(stat_in.at[pl.ds(0, NSEQ - 1)], stat_in.at[pl.ds(0, NSEQ - 1)], st_s).wait()
    for _, c in w_copies:
        c.wait_send()
    for c in w_forwards + o_copies + o_forwards:
        c.wait_send()
    for self_copy, c in p_copies:

        @pl.when(jnp.logical_not(self_copy))
        def _():
            c.wait_send()


def body(
    patches, noise, timesteps, labels, lengths, time_w1, time_w2, label_table, patch_w, mod_w, qkv_w, out_w, head_w
):
    copy_index = lax.axis_index("cfg")
    is_cond = copy_index == 0
    tfreq = time_table(timesteps).astype(jnp.bfloat16)
    time_hidden = jax.nn.silu(jnp.dot(tfreq, time_w1, preferred_element_type=jnp.float32)).astype(jnp.bfloat16)
    time_embed = jnp.dot(time_hidden, time_w2, preferred_element_type=jnp.float32)
    label_rows = label_table.shape[0]
    label_used = jnp.where(is_cond, labels, label_rows - 1)
    one_hot = (label_used[:, None] == jnp.arange(label_rows, dtype=jnp.int32)[None, :]).astype(jnp.bfloat16)
    cond = time_embed + jnp.dot(one_hot, label_table, preferred_element_type=jnp.float32)
    cond_act = jax.nn.silu(cond).astype(jnp.bfloat16)
    mod_part = jnp.dot(cond_act, mod_w, preferred_element_type=jnp.float32)
    modp = jnp.pad(mod_part, ((0, 0), (0, BLK - MODC))).reshape(16, 1, BLK)

    vmem = pl.BlockSpec(memory_space=pltpu.VMEM)
    hbm = pl.BlockSpec(memory_space=pl.ANY)
    bf, f32 = jnp.bfloat16, jnp.float32
    dma = pltpu.SemaphoreType.DMA
    pred, stats = pl.pallas_call(
        kernel,
        out_shape=(
            jax.ShapeDtypeStruct((8, SLOT, 32), f32),
            jax.ShapeDtypeStruct((NSEQ, 1, BLK), f32),
        ),
        in_specs=[pl.BlockSpec(memory_space=pltpu.SMEM), vmem, vmem, hbm, hbm, vmem, vmem, vmem, vmem, vmem, vmem],
        out_specs=(vmem, vmem),
        scratch_shapes=[
            pltpu.VMEM((4, SLOT, 16), bf),
            pltpu.VMEM((NSEQ, SLOT, 16), bf),
            pltpu.VMEM((NDEV, 1, BLK), f32),
            pltpu.VMEM((5, 1, D), f32),
            pltpu.VMEM((3, D, WIN), bf),
            pltpu.VMEM((NREQ, D, ROWS), bf),
            pltpu.VMEM((SEQ_TOTAL, WIN), bf),
            pltpu.VMEM((SEQ_TOTAL, WIN), bf),
            pltpu.VMEM((SEQ_TOTAL, WIN), bf),
            pltpu.VMEM((GROUP, BLK, WIN), bf),
            pltpu.VMEM((GROUP, BLK, WIN), bf),
            pltpu.VMEM((BLK, D), f32),
            pltpu.VMEM((4, SLOT, 32), f32),
            pltpu.VMEM((8, SLOT, 32), f32),
            pltpu.VMEM((1, BLK), f32),
            pltpu.VMEM((NSEQ, 1, BLK), f32),
            pltpu.VMEM((2, 1, 1), f32),
            dma, dma, dma, dma,
            dma((3, 3)), dma((3, 3)), dma((3,)), dma((3,)), dma((3,)),
            dma((3,)), dma((3,)), dma, dma((3,)), dma((3,)),
            dma, dma, dma((8,)), dma, dma, dma,
        ],
        compiler_params=pltpu.CompilerParams(
            collective_id=0, has_side_effects=True, vmem_limit_bytes=56 * 1024 * 1024
        ),
        name="guided_block",
    )(lengths, patches, modp, qkv_w, out_w, head_w, patch_w, *position_factors())

    first_req = lax.axis_index("req") * NREQ
    my_lengths = lax.dynamic_slice_in_dim(lengths, first_req, NREQ, 0)
    my_steps = lax.dynamic_slice_in_dim(timesteps, first_req, NREQ, 0)
    stats = stats.reshape(NREQ, GROUP, BLK)
    norm_values = jnp.sqrt(jnp.sum(stats[:, :, 0], axis=1) / (my_lengths.astype(f32) * D))
    top = stats[:, :, 1:3].reshape(NREQ, HEADS)

    eps_cond, eps_uncond = pred[:NREQ, :, :16], pred[NREQ:, :, :16]
    guided = eps_uncond + guide_scale * (eps_cond - eps_uncond)
    varpart = pred[:NREQ, :, 16:]

    def own_channels(values):
        return lax.dynamic_slice_in_dim(values, copy_index * 8, 8, 2)

    slot_pos = lax.axis_index("seq") * SLOT + jnp.arange(SLOT, dtype=jnp.int32)
    query_ok = slot_pos[None, :] < my_lengths[:, None]
    guided_update = sampler_step(
        own_channels(patches),
        own_channels(noise),
        own_channels(guided),
        own_channels(varpart),
        my_steps.astype(f32)[:, None, None],
        query_ok[:, :, None],
    )
    return (guided_update, norm_values[None, :], top[None, :, :])


def solution(mesh):
    in_specs = (
        P("req", "seq", None),
        P("req", "seq", None),
        P(), P(), P(), P(), P(), P(), P(),
        P(None, ("req", "seq")),
        P("req", None),
        P(None, "req"),
        P(),
    )
    out_specs = (P("req", "seq", "cfg"), P("cfg", "req"), P("cfg", "req", None))
    return jax.shard_map(body, mesh=mesh, in_specs=in_specs, out_specs=out_specs, check_vma=False)
```

```python
import math

import jax
import jax.numpy as jnp
import numpy as np
from jax import lax
from jax.experimental import pallas as pl
from jax.experimental.pallas import tpu as pltpu
from jax.sharding import PartitionSpec as P

HEADS = 16
FREQ = 256
D = 1152
SEQ_TOTAL = 1024
NSEQ = 32
NREQ = 4
NDEV = NSEQ * NREQ
GROUP = 8
SLOT = 32
BLK = 128
WIN = 256
PAIR = 144
HEAD_DIM = 72
ROWS = 288
HALF = 144
MODC = 45
MESH = pl.DeviceIdType.MESH

norm_eps = 1e-06
masked_score = -1e30
guide_scale = 4.0
plan_offset = 0.008
diffusion_steps = 1000.0
INV_ROOT = 1.0 / math.sqrt(HEAD_DIM)
EXP_SCALE = INV_ROOT * math.log2(math.e)


def position_factors():
    half = D // 2
    rates = np.exp(-math.log(10000.0) * np.arange(half) / half)
    coarse = (SLOT * np.arange(NSEQ))[:, None] * rates[None, :]
    fine = np.arange(SLOT)[:, None] * rates[None, :]
    sc, cc, sf, cf = np.sin(coarse), np.cos(coarse), np.sin(fine), np.cos(fine)
    p1 = np.concatenate([sc, cc], axis=1)[:, None, :]
    p2 = np.concatenate([cc, -sc], axis=1)[:, None, :]
    q1 = np.concatenate([cf, cf], axis=1)
    q2 = np.concatenate([sf, sf], axis=1)
    return [jnp.asarray(t.astype(np.float32)) for t in (p1, p2, q1, q2)]


def alpha_bar(steps):
    phase = (steps / diffusion_steps + plan_offset) / (1.0 + plan_offset) * (math.pi / 2.0)
    return jnp.cos(phase) ** 2


def sampler_plan(patches, noise, steps, valid):
    abar = alpha_bar(steps)
    abar_prev = alpha_bar(steps - 1.0)
    beta = 1.0 - abar / abar_prev
    tilde = beta * (1.0 - abar_prev) / (1.0 - abar)
    root_rest, root, log_beta, log_tilde = jnp.sqrt(1.0 - abar), jnp.sqrt(abar), jnp.log(beta), jnp.log(tilde)
    on_start = beta * jnp.sqrt(abar_prev) / (1.0 - abar)
    from_patches = (1.0 - abar_prev) * jnp.sqrt(1.0 - beta) / (1.0 - abar) * patches

    def finish(guided, varpart):
        mean = on_start * ((patches - root_rest * guided) / root) + from_patches
        frac = (varpart + 1.0) * 0.5
        logvar = frac * log_beta + (1.0 - frac) * log_tilde
        return jnp.where(valid, mean + jnp.exp(0.5 * logvar) * noise, 0.0)

    return finish


def layer_norm(values):
    center = values - jnp.mean(values, axis=-1, keepdims=True)
    spread = jnp.mean(center * center, axis=-1, keepdims=True)
    return center * lax.rsqrt(spread + norm_eps)


def silu(values):
    return values / (1.0 + jnp.exp(-values))


NT = (((1,), (1,)), ((), ()))


def kernel(
    len_ref, step_ref, label_ref,
    patches_ref, noise_ref, w1_hbm, w2_hbm, table_hbm, modw_hbm, rates_ref, qkv_hbm, outw_hbm, headw_ref, patchw_ref,
    p1_ref, p2_ref, q1_ref, q2_ref,
    guided_out, norm_out, top_out,
    w1, w2, table, modw, modp,
    pb, patch_all, mod_all, mod_rows, xhat, hid0, wbuf, outbuf, qbuf, kbuf, vbuf, mbuf, mixin, predsend, pred_in,
    stat_send, stat_in, top,
    ld, mod_s, mod_r, pat_s, pat_r, w_s, w_r, wl, wf_s, wf_r, o_s, o_r, ol, of_s, of_r, mx_s, mx_r, pr_s, pr_r, st_s, st_r,
):
    g = lax.axis_index("cfg")
    y = lax.axis_index("req")
    s = lax.axis_index("seq")
    other = 1 - g
    me = y * NSEQ + s
    q = lax.div(s, GROUP)
    j = lax.rem(s, GROUP)

    def remote(src, dst, ssem, rsem, dev):
        return pltpu.make_async_remote_copy(
            src_ref=src, dst_ref=dst, send_sem=ssem, recv_sem=rsem, device_id=dev, device_id_type=MESH
        )

    def wait_bytes(ref, sem):
        pltpu.make_async_copy(ref, ref, sem).wait()

    def each_other(act):
        reqs = [lax.rem(y + dy, NREQ) for dy in range(NREQ)]
        for dy in range(1, NREQ):
            act(reqs[dy], s)

        def step(k, _):
            ts = lax.rem(s + k, NSEQ)
            for ty in reqs:
                act(ty, ts)
            return 0

        lax.fori_loop(1, NSEQ, step, 0)

    bar = pltpu.get_barrier_semaphore()
    each_other(lambda ty, ts: pl.semaphore_signal(bar, inc=1, device_id=(g, ty, ts), device_id_type=MESH))
    for qq in range(NREQ):
        pl.semaphore_signal(bar, inc=1, device_id=(other, y, qq * GROUP + lax.div(s, NREQ)), device_id_type=MESH)
    pl.semaphore_signal(bar, inc=1, device_id=(other, y, s), device_id_type=MESH)

    loads = []
    for i, (src, dst) in enumerate(((w1_hbm, w1), (w2_hbm, w2), (table_hbm, table), (modw_hbm, modw))):
        c = pltpu.make_async_copy(src, dst, ld.at[i])
        c.start()
        loads.append(c)
    col = pl.multiple_of(j * BLK, BLK)
    local_w = []
    for kind in range(3):
        c = pltpu.make_async_copy(
            qkv_hbm.at[:, pl.ds(pl.multiple_of(kind * D + col, BLK), WIN)],
            wbuf.at[kind, pl.ds(pl.multiple_of(ROWS * y, 16), ROWS), :],
            wl.at[kind],
        )
        c.start()
        local_w.append(c)
    local_o = pltpu.make_async_copy(outw_hbm, outbuf.at[pl.ds(pl.multiple_of(ROWS * y, 16), ROWS), :], ol)
    local_o.start()

    for r in range(NREQ):
        pb[r] = jnp.transpose(patches_ref[r]).astype(jnp.bfloat16)

    req_row = lax.broadcasted_iota(jnp.int32, (16, 1), 0)
    times = jnp.zeros((16, 1), jnp.int32)
    used = jnp.zeros((16, 1), jnp.int32)
    for r in range(16):
        times = jnp.where(req_row == r, step_ref[r], times)
        used = jnp.where(req_row == r, label_ref[r], used)
    used = jnp.where(g == 0, used, 1000)
    angles = times.astype(jnp.float32) * rates_ref[...]
    tfreq = jnp.concatenate([jnp.cos(angles), jnp.sin(angles)], axis=1).astype(jnp.bfloat16)
    one_hot = jnp.where(lax.broadcasted_iota(jnp.int32, (16, 1001), 1) == used, 1.0, 0.0).astype(jnp.bfloat16)
    loads[0].wait()
    time_hidden = silu(jnp.dot(tfreq, w1[...], preferred_element_type=jnp.float32)).astype(jnp.bfloat16)
    loads[1].wait()
    cond = jnp.dot(time_hidden, w2[...], preferred_element_type=jnp.float32)
    loads[2].wait()
    cond = cond + jnp.dot(one_hot, table[...], preferred_element_type=jnp.float32)
    cond_act = silu(cond).astype(jnp.bfloat16)
    loads[3].wait()
    mod_part = lax.dot_general(cond_act, modw[...], NT, preferred_element_type=jnp.float32)
    modp[...] = jnp.zeros_like(modp)
    for r in range(16):
        modp[r, :, :MODC] = mod_part[r : r + 1, :]

    pl.semaphore_wait(bar, NDEV - 1 + NREQ + 1)

    def send_patch(k, _):
        d = lax.rem(s + k, NSEQ)
        remote(pb.at[lax.div(d, GROUP)], patch_all.at[s], pat_s, pat_r, (g, y, d)).start()
        return 0

    lax.fori_loop(1, NSEQ, send_patch, 0)

    each_other(
        lambda ty, ts: remote(
            modp.at[ty * NREQ + lax.div(ts, GROUP)], mod_all.at[me], mod_s, mod_r, (g, ty, ts)
        ).start()
    )

    up, down = lax.rem(y + 1, NREQ), lax.rem(y + 3, NREQ)
    onward = lax.rem(y + 1 + 2 * g, NREQ)
    behind = lax.rem(y + 3 + 2 * g, NREQ)
    across = lax.rem(y + 2, NREQ)

    def w_part(ry, core):
        return wbuf.at[:, pl.ds(pl.multiple_of(ROWS * ry + HALF * core, 16), HALF), :]

    def o_part(ry, core):
        return outbuf.at[pl.ds(pl.multiple_of(ROWS * ry + HALF * core, 16), HALF), :]

    for i, ty in enumerate((up, down)):
        for kind in range(3):
            remote(
                qkv_hbm.at[pl.ds(pl.multiple_of(HALF * g, 16), HALF), pl.ds(pl.multiple_of(kind * D + col, BLK), WIN)],
                wbuf.at[kind, pl.ds(pl.multiple_of(ROWS * y + HALF * g, 16), HALF), :],
                w_s.at[i],
                w_r.at[i],
                (g, ty, s),
            ).start()

    mod_all[me] = modp[y * NREQ + q]
    patch_all[s] = pb[q]
    length = len_ref[y * NREQ + q]
    wait_bytes(patch_all.at[pl.ds(0, NSEQ - 1)], pat_r)

    def embed(first_source, count):
        x = patch_all[pl.ds(first_source, count)].reshape(count * SLOT, 16)
        h = jnp.dot(x, patchw_ref[...], preferred_element_type=jnp.float32)
        places = [
            p1_ref[first_source + i] * q1_ref[...] + p2_ref[first_source + i] * q2_ref[...] for i in range(count)
        ]
        return h + jnp.concatenate(places, axis=0)

    def normalise(b, _):
        xhat[pl.ds(pl.multiple_of(b * BLK, BLK), BLK), :] = layer_norm(embed(b * 4, 4))
        return 0

    lax.fori_loop(0, GROUP, normalise, 0)

    wait_bytes(w_part(0, 0), w_r.at[g])
    w_relay = remote(w_part(behind, g), w_part(behind, g), w_s.at[2], w_r.at[2], (g, onward, s))
    w_relay.start()
    w_forwards = [remote(w_part(behind, g), w_part(behind, g), wf_s.at[0], wf_r.at[0], (other, y, s))]
    w_forwards[0].start()
    o_own = o_part(y, g)
    o_mine = outw_hbm.at[pl.ds(pl.multiple_of(HALF * g, 16), HALF), :]
    o_copies = [remote(o_mine, o_own, o_s.at[i], o_r.at[i], (g, ty, s)) for i, ty in enumerate((up, down))]
    for c in o_copies:
        c.start()
    wait_bytes(w_part(0, 0), w_r.at[other])
    w_forwards.append(remote(w_part(onward, g), w_part(onward, g), wf_s.at[1], wf_r.at[1], (other, y, s)))
    w_forwards[1].start()

    wait_bytes(mod_all.at[pl.ds(0, NDEV - 1)], mod_r)
    lane_row = lax.broadcasted_iota(jnp.int32, (1, BLK), 1)
    for tile in range(5 * D // BLK):
        first = (tile * BLK) // MODC
        last = (tile * BLK + BLK - 1) // MODC
        value = None
        for source in range(first, last + 1):
            at = source * MODC - tile * BLK
            piece = mod_all[source]
            if at % BLK:
                piece = pltpu.roll(piece, at % BLK, 1)
            value = piece if value is None else jnp.where(lane_row >= at, piece, value)
        mod_rows[tile // 9, :, (tile % 9) * BLK : (tile % 9 + 1) * BLK] = value
    hid0[...] = embed(j * 4, 4)

    w_relay.wait_recv()
    w_forwards.append(remote(w_part(across, g), w_part(across, g), wf_s.at[2], wf_r.at[2], (other, y, s)))
    w_forwards[2].start()
    for c in local_w:
        c.wait()
    for f in w_forwards:
        f.wait_recv()

    lane = lax.broadcasted_iota(jnp.int32, (1, WIN), 1)
    low = j * 16
    in_a = (lane >= low) & (lane < low + HEAD_DIM)
    in_b = (lane >= low + HEAD_DIM) & (lane < low + PAIR)
    spare = lane == lax.rem(low + PAIR, WIN)

    def project(b, _):
        rows = pl.ds(pl.multiple_of(b * 256, 256), 256)
        normed = (xhat[rows, :] * (1.0 + mod_rows[1]) + mod_rows[0]).astype(jnp.bfloat16)
        qbuf[rows, :] = jnp.dot(normed, wbuf[0], preferred_element_type=jnp.float32).astype(jnp.bfloat16)
        keys = jnp.dot(normed, wbuf[1], preferred_element_type=jnp.float32)
        place = b * 256 + lax.broadcasted_iota(jnp.int32, (256, 1), 0)
        bias = jnp.where(place < length, 0.0, masked_score)
        kbuf[rows, :] = jnp.where(spare, bias, keys).astype(jnp.bfloat16)
        vbuf[rows, :] = jnp.dot(normed, wbuf[2], preferred_element_type=jnp.float32).astype(jnp.bfloat16)
        return 0

    lax.fori_loop(0, 4, project, 0)

    wait_bytes(o_part(0, 0), o_r.at[g])
    o_relay = remote(o_part(behind, g), o_part(behind, g), o_s.at[2], o_r.at[2], (g, onward, s))
    o_relay.start()
    o_forwards = [remote(o_part(behind, g), o_part(behind, g), of_s.at[0], of_r.at[0], (other, y, s))]
    o_forwards[0].start()
    wait_bytes(o_part(0, 0), o_r.at[other])
    o_forwards.append(remote(o_part(onward, g), o_part(onward, g), of_s.at[1], of_r.at[1], (other, y, s)))
    o_forwards[1].start()
    o_forwards.append(remote(o_part(across, g), o_part(across, g), of_s.at[2], of_r.at[2], (other, y, s)))

    top[...] = jnp.full_like(top, masked_score)

    def attend(k, _):
        b = lax.rem(j + k, GROUP)
        rows = pl.ds(pl.multiple_of(b * BLK, BLK), BLK)
        query = qbuf[rows, :].astype(jnp.float32)
        live = b * BLK + lax.broadcasted_iota(jnp.int32, (BLK, 1), 0) < length
        mixed = jnp.zeros((BLK, WIN), jnp.float32)
        for head, inside in enumerate((in_a, in_b)):
            mine = jnp.where(inside, query, jnp.where(spare, 1.0, 0.0)).astype(jnp.bfloat16)
            raw = lax.dot_general(mine, kbuf[...], NT, preferred_element_type=jnp.float32)
            peak = jnp.max(raw, axis=1, keepdims=True)
            expo = jnp.exp2((raw - peak) * EXP_SCALE)
            total = jnp.sum(expo, axis=1, keepdims=True)
            summed = jnp.dot(expo.astype(jnp.bfloat16), vbuf[...], preferred_element_type=jnp.float32)
            mixed = jnp.where(inside, summed * (1.0 / total), mixed)
            best = jnp.max(jnp.where(live, peak, masked_score), axis=0, keepdims=True)
            top[head] = jnp.maximum(top[head], best)
        mbuf[b] = mixed.astype(jnp.bfloat16)

        @pl.when(k < GROUP)
        def _():
            remote(mbuf.at[b], mixin.at[j], mx_s, mx_r, (g, y, q * GROUP + b)).start()

        @pl.when(k == GROUP - 2)
        def _():
            o_relay.wait_recv()
            o_forwards[2].start()

        return 0

    lax.fori_loop(1, GROUP + 1, attend, 0)
    mixin[j] = mbuf[j]
    local_o.wait()
    for f in o_forwards:
        f.wait_recv()
    wait_bytes(mixin.at[pl.ds(0, GROUP - 1)], mx_r)

    tiles = []
    for t in range(9):
        tile = mixin[t, :, :BLK] if t < GROUP else None
        if t > 0:
            rest = mixin[t - 1, :, BLK:]
            tile = rest if tile is None else tile + rest
        tiles.append(tile)
    mixed_all = jnp.concatenate(tiles, axis=1)
    attended = lax.dot_general(mixed_all, outbuf[...], NT, preferred_element_type=jnp.float32)
    hidden1 = hid0[...] + mod_rows[2] * attended
    place = j * BLK + lax.broadcasted_iota(jnp.int32, (BLK, 1), 0)
    squares = jnp.sum(
        jnp.sum(jnp.where(place < length, hidden1 * hidden1, 0.0), axis=1, keepdims=True), axis=0, keepdims=True
    )
    stat = jnp.where(
        lane_row == 2 * j,
        top[0] * INV_ROOT,
        jnp.where(lane_row == 2 * j + 1, top[1] * INV_ROOT, jnp.where(lane_row == HEADS, squares, 0.0)),
    )
    stat_send[...] = stat

    def send_stat(k, _):
        d = lax.rem(s + k, NSEQ)
        remote(stat_send, stat_in.at[s], st_s, st_r, (g, y, d)).start()
        return 0

    lax.fori_loop(1, NSEQ, send_stat, 0)
    stat_in[s] = stat

    normed2 = (layer_norm(hidden1) * (1.0 + mod_rows[4]) + mod_rows[3]).astype(jnp.bfloat16)
    prediction = lax.dot_general(headw_ref[...], normed2, NT, preferred_element_type=jnp.float32)
    slot = g * NREQ + q
    p_copies = []
    for i in range(NREQ):
        for gg in range(2):
            for part in range(2):
                predsend[gg * NREQ + i, 8 * part : 8 * part + 8, :] = prediction[
                    16 * part + 8 * gg : 16 * part + 8 * gg + 8, SLOT * i : SLOT * i + SLOT
                ]
            ts = j * NREQ + i
            self_copy = (ts == s) & (g == gg)
            c = remote(predsend.at[gg * NREQ + i], pred_in.at[slot], pr_s.at[i * 2 + gg], pr_r, (gg, y, ts))
            p_copies.append((self_copy, c))

            @pl.when(jnp.logical_not(self_copy))
            def _():
                c.start()

            @pl.when(self_copy)
            def _():
                pltpu.make_async_copy(predsend.at[gg * NREQ + i], pred_in.at[slot], pr_r).start()

    shape = (NREQ, 8, SLOT)
    which = lax.broadcasted_iota(jnp.int32, shape, 0)
    steps = jnp.zeros(shape, jnp.int32)
    limits = jnp.zeros(shape, jnp.int32)
    for r in range(NREQ):
        steps = jnp.where(which == r, step_ref[y * NREQ + r], steps)
        limits = jnp.where(which == r, len_ref[y * NREQ + r], limits)
    valid = s * SLOT + lax.broadcasted_iota(jnp.int32, shape, 2) < limits
    channels = pl.ds(pl.multiple_of(g * 8, 8), 8)
    own_patches = patches_ref[:, channels, :]
    own_noise = noise_ref[:, channels, :]
    finish = sampler_plan(own_patches, own_noise, steps.astype(jnp.float32), valid)

    wait_bytes(pred_in, pr_r)
    eps_cond, eps_uncond = pred_in[:NREQ, :8, :], pred_in[NREQ:, :8, :]
    guided = eps_uncond + guide_scale * (eps_cond - eps_uncond)
    guided_out[...] = finish(guided, pred_in[:NREQ, 8:, :])

    wait_bytes(stat_in.at[pl.ds(0, NSEQ - 1)], st_r)
    for r in range(NREQ):
        row = stat_in[r * GROUP]
        for i in range(1, GROUP):
            row = row + stat_in[r * GROUP + i]
        top_out[r : r + 1, :] = row[:, :HEADS]
        count = jnp.full((1, 1), len_ref[y * NREQ + r], jnp.int32).astype(jnp.float32) * D
        norm_out[:, r : r + 1] = jnp.sqrt(row[:, HEADS : HEADS + 1] / count)

    wait_bytes(mod_all.at[pl.ds(0, NDEV - 1)], mod_s)
    wait_bytes(patch_all.at[pl.ds(0, NSEQ - 1)], pat_s)
    wait_bytes(mixin.at[pl.ds(0, GROUP - 1)], mx_s)
    wait_bytes(stat_in.at[pl.ds(0, NSEQ - 1)], st_s)
    for i in range(2):
        wait_bytes(w_part(0, 0), w_s.at[i])
    for c in [w_relay, o_relay] + w_forwards + o_copies + o_forwards:
        c.wait_send()
    for self_copy, c in p_copies:

        @pl.when(jnp.logical_not(self_copy))
        def _():
            c.wait_send()


def body(
    patches, noise, timesteps, labels, lengths, time_w1, time_w2, label_table, patch_w, mod_w, qkv_w, out_w, head_w
):
    vmem = pl.BlockSpec(memory_space=pltpu.VMEM)
    hbm = pl.BlockSpec(memory_space=pl.ANY)
    smem = pl.BlockSpec(memory_space=pltpu.SMEM)
    bf, f32 = jnp.bfloat16, jnp.float32
    dma = pltpu.SemaphoreType.DMA
    rates = np.exp(-math.log(10000.0) * np.arange(FREQ // 2) / (FREQ // 2)).astype(np.float32)[None, :]
    guided, norms, top = pl.pallas_call(
        kernel,
        out_shape=(
            jax.ShapeDtypeStruct((NREQ, 8, SLOT), f32),
            jax.ShapeDtypeStruct((1, NREQ), f32),
            jax.ShapeDtypeStruct((NREQ, HEADS), f32),
        ),
        in_specs=[smem] * 3 + [vmem] * 2 + [hbm] * 4 + [vmem] + [hbm] * 2 + [vmem] * 6,
        out_specs=(vmem, vmem, vmem),
        scratch_shapes=[
            pltpu.VMEM((FREQ, D), bf),
            pltpu.VMEM((D, D), bf),
            pltpu.VMEM((1001, D), bf),
            pltpu.VMEM((MODC, D), bf),
            pltpu.VMEM((16, 1, BLK), f32),
            pltpu.VMEM((4, SLOT, 16), bf),
            pltpu.VMEM((NSEQ, SLOT, 16), bf),
            pltpu.VMEM((NDEV, 1, BLK), f32),
            pltpu.VMEM((5, 1, D), f32),
            pltpu.VMEM((SEQ_TOTAL, D), f32),
            pltpu.VMEM((BLK, D), f32),
            pltpu.VMEM((3, D, WIN), bf),
            pltpu.VMEM((D, D), bf),
            pltpu.VMEM((SEQ_TOTAL, WIN), bf),
            pltpu.VMEM((SEQ_TOTAL, WIN), bf),
            pltpu.VMEM((SEQ_TOTAL, WIN), bf),
            pltpu.VMEM((GROUP, BLK, WIN), bf),
            pltpu.VMEM((GROUP, BLK, WIN), bf),
            pltpu.VMEM((8, 16, SLOT), f32),
            pltpu.VMEM((8, 16, SLOT), f32),
            pltpu.VMEM((1, BLK), f32),
            pltpu.VMEM((NSEQ, 1, BLK), f32),
            pltpu.VMEM((2, 1, 1), f32),
            dma((4,)), dma, dma, dma, dma,
            dma((3,)), dma((3,)), dma((3,)), dma((3,)), dma((3,)),
            dma((3,)), dma((3,)), dma, dma((3,)), dma((3,)),
            dma, dma, dma((8,)), dma, dma, dma,
        ],
        compiler_params=pltpu.CompilerParams(
            collective_id=0, has_side_effects=True, vmem_limit_bytes=56 * 1024 * 1024
        ),
        name="guided_block",
    )(
        lengths, timesteps, labels,
        jnp.transpose(patches, (0, 2, 1)), jnp.transpose(noise, (0, 2, 1)),
        time_w1, time_w2, label_table, jnp.transpose(mod_w), jnp.asarray(rates), qkv_w, jnp.transpose(out_w),
        jnp.transpose(head_w), patch_w, *position_factors(),
    )
    return (jnp.transpose(guided, (0, 2, 1)), norms, top[None, :, :])


def solution(mesh):
    in_specs = (
        P("req", "seq", None),
        P("req", "seq", None),
        P(), P(), P(), P(), P(), P(), P(),
        P(None, ("req", "seq")),
        P("req", None),
        P(None, "req"),
        P(),
    )
    out_specs = (P("req", "seq", "cfg"), P("cfg", "req"), P("cfg", "req", None))
    return jax.shard_map(body, mesh=mesh, in_specs=in_specs, out_specs=out_specs, check_vma=False)
```

```python
import math

import jax
import jax.numpy as jnp
import numpy as np
from jax import lax
from jax.experimental import pallas as pl
from jax.experimental.pallas import tpu as pltpu
from jax.sharding import PartitionSpec as P

HEADS = 16
FREQ = 256
D = 1152
SEQ_TOTAL = 1024
NSEQ = 32
NREQ = 4
NX = 4
NZ = 8
GROUP = 8
SLOT = 32
BLK = 128
WIN = 256
PAIR = 144
HEAD_DIM = 72
ROWS = 288
HALF = 144
MODC = 45
MESH = pl.DeviceIdType.MESH

norm_eps = 1e-06
masked_score = -1e30
guide_scale = 4.0
plan_offset = 0.008
diffusion_steps = 1000.0
INV_ROOT = 1.0 / math.sqrt(HEAD_DIM)
EXP_SCALE = INV_ROOT * math.log2(math.e)


def position_factors():
    half = D // 2
    rates = np.exp(-math.log(10000.0) * np.arange(half) / half)
    coarse = (SLOT * np.arange(NSEQ))[:, None] * rates[None, :]
    fine = np.arange(SLOT)[:, None] * rates[None, :]
    sc, cc, sf, cf = np.sin(coarse), np.cos(coarse), np.sin(fine), np.cos(fine)
    p1 = np.concatenate([sc, cc], axis=1)[:, None, :]
    p2 = np.concatenate([cc, -sc], axis=1)[:, None, :]
    q1 = np.concatenate([cf, cf], axis=1)
    q2 = np.concatenate([sf, sf], axis=1)
    return [jnp.asarray(t.astype(np.float32)) for t in (p1, p2, q1, q2)]


def alpha_bar(steps):
    phase = (steps / diffusion_steps + plan_offset) / (1.0 + plan_offset) * (math.pi / 2.0)
    return jnp.cos(phase) ** 2


def sampler_step(patches, noise, guided, varpart, steps, valid):
    abar = alpha_bar(steps)
    abar_prev = alpha_bar(steps - 1.0)
    beta = 1.0 - abar / abar_prev
    start = (patches - jnp.sqrt(1.0 - abar) * guided) / jnp.sqrt(abar)
    mean = (
        beta * jnp.sqrt(abar_prev) / (1.0 - abar) * start
        + (1.0 - abar_prev) * jnp.sqrt(1.0 - beta) / (1.0 - abar) * patches
    )
    tilde = beta * (1.0 - abar_prev) / (1.0 - abar)
    frac = (varpart + 1.0) * 0.5
    logvar = frac * jnp.log(beta) + (1.0 - frac) * jnp.log(tilde)
    return jnp.where(valid, mean + jnp.exp(0.5 * logvar) * noise, 0.0)


def layer_norm(values):
    center = values - jnp.mean(values, axis=-1, keepdims=True)
    spread = jnp.mean(center * center, axis=-1, keepdims=True)
    return center * lax.rsqrt(spread + norm_eps)


def silu(values):
    return values / (1.0 + jnp.exp(-values))


NT = (((1,), (1,)), ((), ()))


def kernel(
    len_ref, step_ref, label_ref,
    patches_ref, w1_hbm, w2_hbm, table_hbm, modw_hbm, rates_ref, qkv_hbm, outw_hbm, headw_ref, patchw_ref,
    p1_ref, p2_ref, q1_ref, q2_ref,
    pred_out, stat_out,
    w1, w2, table, modw, modp,
    pb, patch_x, patch_m, patch_z, mod_y, mod_x, mod_z, mod_rows, xhat, hid0, wbuf, outbuf, qbuf, kbuf, vbuf, mbuf, mixin, predsend, pred_in,
    stat_send, stat_in, top,
    ld, my_s, my_r, mx_s2, mx_r2, mz_s, mz_r, px_s, px_r, pz_s, pz_r, w_s, w_r, wl, wf_s, wf_r, o_s, o_r, ol, of_s, of_r, mx_s, mx_r, pr_s, pr_r, st_s, st_r,
):
    g = lax.axis_index("cfg")
    y = lax.axis_index("req")
    s = lax.axis_index("seq")
    other = 1 - g
    z, x = lax.div(s, NX), lax.rem(s, NX)
    q = lax.div(s, GROUP)
    j = lax.rem(s, GROUP)

    def remote(src, dst, ssem, rsem, dev):
        return pltpu.make_async_remote_copy(
            src_ref=src, dst_ref=dst, send_sem=ssem, recv_sem=rsem, device_id=dev, device_id_type=MESH
        )

    def wait_bytes(ref, sem):
        pltpu.make_async_copy(ref, ref, sem).wait()

    bar = pltpu.get_barrier_semaphore()
    in_block = 4 * z + NX - 8 * lax.rem(z, 2)
    near = [(g, lax.rem(y + k, NREQ), s) for k in range(1, NREQ)]
    near += [(g, y, z * NX + lax.rem(x + k, NX)) for k in range(1, NX)]
    near += [(g, y, lax.rem(z + k, NZ) * NX + x) for k in range(1, NZ)]
    near += [(g, y, in_block + lax.rem(x + k, NX)) for k in range(1, NX)]
    near += [(other, y, s)]
    for device in near:
        pl.semaphore_signal(bar, inc=1, device_id=device, device_id_type=MESH)

    loads = []
    for i, (src, dst) in enumerate(((w1_hbm, w1), (w2_hbm, w2), (table_hbm, table), (modw_hbm, modw))):
        c = pltpu.make_async_copy(src, dst, ld.at[i])
        c.start()
        loads.append(c)
    col = pl.multiple_of(j * BLK, BLK)
    local_w = []
    for kind in range(3):
        c = pltpu.make_async_copy(
            qkv_hbm.at[:, pl.ds(pl.multiple_of(kind * D + col, BLK), WIN)],
            wbuf.at[kind, pl.ds(pl.multiple_of(ROWS * y, 16), ROWS), :],
            wl.at[kind],
        )
        c.start()
        local_w.append(c)
    local_o = pltpu.make_async_copy(outw_hbm, outbuf.at[pl.ds(pl.multiple_of(ROWS * y, 16), ROWS), :], ol)
    local_o.start()

    pb[...] = patches_ref[...].astype(jnp.bfloat16)

    req_row = lax.broadcasted_iota(jnp.int32, (16, 1), 0)
    times = jnp.zeros((16, 1), jnp.int32)
    used = jnp.zeros((16, 1), jnp.int32)
    for r in range(16):
        times = jnp.where(req_row == r, step_ref[r], times)
        used = jnp.where(req_row == r, label_ref[r], used)
    used = jnp.where(g == 0, used, 1000)
    angles = times.astype(jnp.float32) * rates_ref[...]
    tfreq = jnp.concatenate([jnp.cos(angles), jnp.sin(angles)], axis=1).astype(jnp.bfloat16)
    one_hot = jnp.where(lax.broadcasted_iota(jnp.int32, (16, 1001), 1) == used, 1.0, 0.0).astype(jnp.bfloat16)
    loads[0].wait()
    time_hidden = silu(jnp.dot(tfreq, w1[...], preferred_element_type=jnp.float32)).astype(jnp.bfloat16)
    loads[1].wait()
    cond = jnp.dot(time_hidden, w2[...], preferred_element_type=jnp.float32)
    loads[2].wait()
    cond = cond + jnp.dot(one_hot, table[...], preferred_element_type=jnp.float32)
    cond_act = silu(cond).astype(jnp.bfloat16)
    loads[3].wait()
    mod_part = lax.dot_general(cond_act, modw[...], NT, preferred_element_type=jnp.float32)
    modp[...] = jnp.zeros_like(modp)
    for r in range(16):
        modp[r, :, :MODC] = mod_part[r : r + 1, :]

    pl.semaphore_wait(bar, len(near))

    for k in range(1, NREQ):
        ty = lax.rem(y + k, NREQ)
        remote(modp.at[pl.ds(ty * NREQ, NREQ)], mod_y.at[:, y], my_s, my_r, (g, ty, s)).start()
    for k in range(1, NX):
        remote(pb, patch_x.at[x], px_s, px_r, (g, y, z * NX + lax.rem(x + k, NX))).start()

    up, down = lax.rem(y + 1, NREQ), lax.rem(y + 3, NREQ)
    onward = lax.rem(y + 1 + 2 * g, NREQ)
    behind = lax.rem(y + 3 + 2 * g, NREQ)
    across = lax.rem(y + 2, NREQ)

    def w_part(ry, core):
        return wbuf.at[:, pl.ds(pl.multiple_of(ROWS * ry + HALF * core, 16), HALF), :]

    def o_part(ry, core):
        return outbuf.at[pl.ds(pl.multiple_of(ROWS * ry + HALF * core, 16), HALF), :]

    for i, ty in enumerate((up, down)):
        for kind in range(3):
            remote(
                qkv_hbm.at[pl.ds(pl.multiple_of(HALF * g, 16), HALF), pl.ds(pl.multiple_of(kind * D + col, BLK), WIN)],
                wbuf.at[kind, pl.ds(pl.multiple_of(ROWS * y + HALF * g, 16), HALF), :],
                w_s.at[i],
                w_r.at[i],
                (g, ty, s),
            ).start()

    mod_y[:, y] = modp[pl.ds(y * NREQ, NREQ)]
    patch_x[x] = pb[...]
    length = len_ref[y * NREQ + q]

    wait_bytes(mod_y.at[pl.ds(0, NREQ - 1)], my_r)
    for k in range(1, NX):
        remote(mod_y, mod_x.at[:, x], mx_s2, mx_r2, (g, y, z * NX + lax.rem(x + k, NX))).start()
    mod_x[:, x] = mod_y[...]
    wait_bytes(patch_x.at[pl.ds(0, NX - 1)], px_r)
    for r in range(NREQ):
        patch_m[r] = jnp.concatenate([patch_x[i, r] for i in range(NX)], axis=1)
    for k in range(1, NZ):
        tz = lax.rem(z + k, NZ)
        remote(patch_m.at[lax.div(tz, 2)], patch_z.at[z], pz_s, pz_r, (g, y, tz * NX + x)).start()
    patch_z[z] = patch_m[q]
    wait_bytes(mod_x.at[pl.ds(0, NX - 1)], mx_r2)
    for k in range(1, NZ):
        tz = lax.rem(z + k, NZ)
        remote(mod_x.at[lax.div(tz, 2)], mod_z.at[z], mz_s, mz_r, (g, y, tz * NX + x)).start()
    mod_z[z] = mod_x[q]

    def embed(b):
        h = lax.dot_general(patch_z[b], patchw_ref[...], (((0,), (0,)), ((), ())), preferred_element_type=jnp.float32)
        places = [p1_ref[b * 4 + i] * q1_ref[...] + p2_ref[b * 4 + i] * q2_ref[...] for i in range(4)]
        return h + jnp.concatenate(places, axis=0)

    def normalise(b, _):
        xhat[pl.ds(pl.multiple_of(b * BLK, BLK), BLK), :] = layer_norm(embed(b))
        return 0

    wait_bytes(w_part(0, 0), w_r.at[g])
    w_relay = remote(w_part(behind, g), w_part(behind, g), w_s.at[2], w_r.at[2], (g, onward, s))
    w_relay.start()
    w_forwards = [remote(w_part(behind, g), w_part(behind, g), wf_s.at[0], wf_r.at[0], (other, y, s))]
    w_forwards[0].start()
    o_own = o_part(y, g)
    o_mine = outw_hbm.at[pl.ds(pl.multiple_of(HALF * g, 16), HALF), :]
    o_copies = [remote(o_mine, o_own, o_s.at[i], o_r.at[i], (g, ty, s)) for i, ty in enumerate((up, down))]
    for c in o_copies:
        c.start()
    wait_bytes(w_part(0, 0), w_r.at[other])
    w_forwards.append(remote(w_part(onward, g), w_part(onward, g), wf_s.at[1], wf_r.at[1], (other, y, s)))
    w_forwards[1].start()

    wait_bytes(patch_z.at[pl.ds(0, NZ - 1)], pz_r)
    lax.fori_loop(0, GROUP, normalise, 0)

    wait_bytes(mod_z.at[pl.ds(0, NZ - 1)], mz_r)
    lane_row = lax.broadcasted_iota(jnp.int32, (1, BLK), 1)
    for tile in range(5 * D // BLK):
        first = (tile * BLK) // MODC
        last = (tile * BLK + BLK - 1) // MODC
        value = None
        for source in range(first, last + 1):
            at = source * MODC - tile * BLK
            piece = mod_z[source % NSEQ // NX, source % NX, source // NSEQ]
            if at % BLK:
                piece = pltpu.roll(piece, at % BLK, 1)
            value = piece if value is None else jnp.where(lane_row >= at, piece, value)
        mod_rows[tile // 9, :, (tile % 9) * BLK : (tile % 9 + 1) * BLK] = value
    hid0[...] = embed(j)

    w_relay.wait_recv()
    w_forwards.append(remote(w_part(across, g), w_part(across, g), wf_s.at[2], wf_r.at[2], (other, y, s)))
    w_forwards[2].start()
    for c in local_w:
        c.wait()
    for f in w_forwards:
        f.wait_recv()

    lane = lax.broadcasted_iota(jnp.int32, (1, WIN), 1)
    low = j * 16
    in_a = (lane >= low) & (lane < low + HEAD_DIM)
    in_b = (lane >= low + HEAD_DIM) & (lane < low + PAIR)
    spare = lane == lax.rem(low + PAIR, WIN)

    def project(b, _):
        rows = pl.ds(pl.multiple_of(b * 256, 256), 256)
        normed = (xhat[rows, :] * (1.0 + mod_rows[1]) + mod_rows[0]).astype(jnp.bfloat16)
        qbuf[rows, :] = jnp.dot(normed, wbuf[0], preferred_element_type=jnp.float32).astype(jnp.bfloat16)
        keys = jnp.dot(normed, wbuf[1], preferred_element_type=jnp.float32)
        place = b * 256 + lax.broadcasted_iota(jnp.int32, (256, 1), 0)
        bias = jnp.where(place < length, 0.0, masked_score)
        kbuf[rows, :] = jnp.where(spare, bias, keys).astype(jnp.bfloat16)
        vbuf[rows, :] = jnp.dot(normed, wbuf[2], preferred_element_type=jnp.float32).astype(jnp.bfloat16)
        return 0

    lax.fori_loop(0, 4, project, 0)

    wait_bytes(o_part(0, 0), o_r.at[g])
    o_relay = remote(o_part(behind, g), o_part(behind, g), o_s.at[2], o_r.at[2], (g, onward, s))
    o_relay.start()
    o_forwards = [remote(o_part(behind, g), o_part(behind, g), of_s.at[0], of_r.at[0], (other, y, s))]
    o_forwards[0].start()
    wait_bytes(o_part(0, 0), o_r.at[other])
    o_forwards.append(remote(o_part(onward, g), o_part(onward, g), of_s.at[1], of_r.at[1], (other, y, s)))
    o_forwards[1].start()
    o_forwards.append(remote(o_part(across, g), o_part(across, g), of_s.at[2], of_r.at[2], (other, y, s)))

    top[...] = jnp.full_like(top, masked_score)

    def attend(k, _):
        b = lax.rem(j + k, GROUP)
        rows = pl.ds(pl.multiple_of(b * BLK, BLK), BLK)
        query = qbuf[rows, :].astype(jnp.float32)
        live = b * BLK + lax.broadcasted_iota(jnp.int32, (BLK, 1), 0) < length
        mixed = jnp.zeros((BLK, WIN), jnp.float32)
        for head, inside in enumerate((in_a, in_b)):
            mine = jnp.where(inside, query, jnp.where(spare, 1.0, 0.0)).astype(jnp.bfloat16)
            raw = lax.dot_general(mine, kbuf[...], NT, preferred_element_type=jnp.float32)
            peak = jnp.max(raw, axis=1, keepdims=True)
            expo = jnp.exp2((raw - peak) * EXP_SCALE)
            total = jnp.sum(expo, axis=1, keepdims=True)
            summed = jnp.dot(expo.astype(jnp.bfloat16), vbuf[...], preferred_element_type=jnp.float32)
            mixed = jnp.where(inside, summed * (1.0 / total), mixed)
            best = jnp.max(jnp.where(live, peak, masked_score), axis=0, keepdims=True)
            top[head] = jnp.maximum(top[head], best)
        mbuf[b] = mixed.astype(jnp.bfloat16)

        @pl.when(k < GROUP)
        def _():
            remote(mbuf.at[b], mixin.at[j], mx_s, mx_r, (g, y, q * GROUP + b)).start()

        @pl.when(k == GROUP - 2)
        def _():
            o_relay.wait_recv()
            o_forwards[2].start()

        return 0

    lax.fori_loop(1, GROUP + 1, attend, 0)
    mixin[j] = mbuf[j]
    local_o.wait()
    for f in o_forwards:
        f.wait_recv()
    wait_bytes(mixin.at[pl.ds(0, GROUP - 1)], mx_r)

    tiles = []
    for t in range(9):
        tile = mixin[t, :, :BLK] if t < GROUP else None
        if t > 0:
            rest = mixin[t - 1, :, BLK:]
            tile = rest if tile is None else tile + rest
        tiles.append(tile)
    mixed_all = jnp.concatenate(tiles, axis=1)
    attended = lax.dot_general(mixed_all, outbuf[...], NT, preferred_element_type=jnp.float32)
    hidden1 = hid0[...] + mod_rows[2] * attended
    place = j * BLK + lax.broadcasted_iota(jnp.int32, (BLK, 1), 0)
    squares = jnp.sum(
        jnp.sum(jnp.where(place < length, hidden1 * hidden1, 0.0), axis=1, keepdims=True), axis=0, keepdims=True
    )
    stat = jnp.where(
        lane_row == 2 * j,
        top[0] * INV_ROOT,
        jnp.where(lane_row == 2 * j + 1, top[1] * INV_ROOT, jnp.where(lane_row == HEADS, squares, 0.0)),
    )
    stat_send[...] = stat

    def send_stat(k, _):
        d = lax.rem(s + k, NSEQ)
        remote(stat_send, stat_in.at[s], st_s, st_r, (g, y, d)).start()
        return 0

    lax.fori_loop(1, NSEQ, send_stat, 0)
    stat_in[s] = stat

    normed2 = (layer_norm(hidden1) * (1.0 + mod_rows[4]) + mod_rows[3]).astype(jnp.bfloat16)
    prediction = lax.dot_general(headw_ref[...], normed2, NT, preferred_element_type=jnp.float32)
    slot = g * NREQ + q
    p_copies = []
    for i in range(NREQ):
        for gg in range(2):
            for part in range(2):
                predsend[gg * NREQ + i, 8 * part : 8 * part + 8, :] = prediction[
                    16 * part + 8 * gg : 16 * part + 8 * gg + 8, SLOT * i : SLOT * i + SLOT
                ]
            ts = j * NREQ + i
            self_copy = (ts == s) & (g == gg)
            c = remote(predsend.at[gg * NREQ + i], pred_in.at[slot], pr_s.at[i * 2 + gg], pr_r, (gg, y, ts))
            p_copies.append((self_copy, c))

            @pl.when(jnp.logical_not(self_copy))
            def _():
                c.start()

            @pl.when(self_copy)
            def _():
                pltpu.make_async_copy(predsend.at[gg * NREQ + i], pred_in.at[slot], pr_r).start()

    wait_bytes(pred_in, pr_r)
    wait_bytes(stat_in.at[pl.ds(0, NSEQ - 1)], st_r)
    pred_out[...] = pred_in[...]
    stat_out[...] = stat_in[...]

    wait_bytes(mod_y.at[pl.ds(0, NREQ - 1)], my_s)
    wait_bytes(mod_x.at[pl.ds(0, NX - 1)], mx_s2)
    wait_bytes(mod_z.at[pl.ds(0, NZ - 1)], mz_s)
    wait_bytes(patch_x.at[pl.ds(0, NX - 1)], px_s)
    wait_bytes(patch_z.at[pl.ds(0, NZ - 1)], pz_s)
    wait_bytes(mixin.at[pl.ds(0, GROUP - 1)], mx_s)
    wait_bytes(stat_in.at[pl.ds(0, NSEQ - 1)], st_s)
    for i in range(2):
        wait_bytes(w_part(0, 0), w_s.at[i])
    for c in [w_relay, o_relay] + w_forwards + o_copies + o_forwards:
        c.wait_send()
    for self_copy, c in p_copies:

        @pl.when(jnp.logical_not(self_copy))
        def _():
            c.wait_send()


def finish(len_ref, step_ref, patches_ref, noise_ref, pred_ref, stat_ref, guided_out, norm_out, top_out):
    g = lax.axis_index("cfg")
    y = lax.axis_index("req")
    s = lax.axis_index("seq")
    shape = (NREQ, 8, SLOT)
    which = lax.broadcasted_iota(jnp.int32, shape, 0)
    steps = jnp.zeros(shape, jnp.int32)
    limits = jnp.zeros(shape, jnp.int32)
    for r in range(NREQ):
        steps = jnp.where(which == r, step_ref[y * NREQ + r], steps)
        limits = jnp.where(which == r, len_ref[y * NREQ + r], limits)
    valid = s * SLOT + lax.broadcasted_iota(jnp.int32, shape, 2) < limits
    channels = pl.ds(pl.multiple_of(g * 8, 8), 8)
    eps_cond, eps_uncond = pred_ref[:NREQ, :8, :], pred_ref[NREQ:, :8, :]
    guided = eps_uncond + guide_scale * (eps_cond - eps_uncond)
    guided_out[...] = sampler_step(
        patches_ref[:, channels, :], noise_ref[:, channels, :], guided, pred_ref[:NREQ, 8:, :],
        steps.astype(jnp.float32), valid,
    )
    for r in range(NREQ):
        row = stat_ref[r * GROUP]
        for i in range(1, GROUP):
            row = row + stat_ref[r * GROUP + i]
        top_out[r : r + 1, :] = row[:, :HEADS]
        count = jnp.full((1, 1), len_ref[y * NREQ + r], jnp.int32).astype(jnp.float32) * D
        norm_out[:, r : r + 1] = jnp.sqrt(row[:, HEADS : HEADS + 1] / count)


def body(
    patches, noise, timesteps, labels, lengths, time_w1, time_w2, label_table, patch_w, mod_w, qkv_w, out_w, head_w
):
    vmem = pl.BlockSpec(memory_space=pltpu.VMEM)
    hbm = pl.BlockSpec(memory_space=pl.ANY)
    smem = pl.BlockSpec(memory_space=pltpu.SMEM)
    bf, f32 = jnp.bfloat16, jnp.float32
    dma = pltpu.SemaphoreType.DMA
    rates = np.exp(-math.log(10000.0) * np.arange(FREQ // 2) / (FREQ // 2)).astype(np.float32)[None, :]
    patches_t, noise_t = jnp.transpose(patches, (0, 2, 1)), jnp.transpose(noise, (0, 2, 1))
    pred, stats = pl.pallas_call(
        kernel,
        out_shape=(
            jax.ShapeDtypeStruct((8, 16, SLOT), f32),
            jax.ShapeDtypeStruct((NSEQ, 1, BLK), f32),
        ),
        in_specs=[smem] * 3 + [vmem] + [hbm] * 4 + [vmem] + [hbm] * 2 + [vmem] * 6,
        out_specs=(vmem, vmem),
        scratch_shapes=[
            pltpu.VMEM((FREQ, D), bf),
            pltpu.VMEM((D, D), bf),
            pltpu.VMEM((1001, D), bf),
            pltpu.VMEM((MODC, D), bf),
            pltpu.VMEM((16, 1, BLK), f32),
            pltpu.VMEM((NREQ, 16, SLOT), bf),
            pltpu.VMEM((NX, NREQ, 16, SLOT), bf),
            pltpu.VMEM((NREQ, 16, BLK), bf),
            pltpu.VMEM((NZ, 16, BLK), bf),
            pltpu.VMEM((NREQ, NREQ, 1, BLK), f32),
            pltpu.VMEM((NREQ, NX, NREQ, 1, BLK), f32),
            pltpu.VMEM((NZ, NX, NREQ, 1, BLK), f32),
            pltpu.VMEM((5, 1, D), f32),
            pltpu.VMEM((SEQ_TOTAL, D), f32),
            pltpu.VMEM((BLK, D), f32),
            pltpu.VMEM((3, D, WIN), bf),
            pltpu.VMEM((D, D), bf),
            pltpu.VMEM((SEQ_TOTAL, WIN), bf),
            pltpu.VMEM((SEQ_TOTAL, WIN), bf),
            pltpu.VMEM((SEQ_TOTAL, WIN), bf),
            pltpu.VMEM((GROUP, BLK, WIN), bf),
            pltpu.VMEM((GROUP, BLK, WIN), bf),
            pltpu.VMEM((8, 16, SLOT), f32),
            pltpu.VMEM((8, 16, SLOT), f32),
            pltpu.VMEM((1, BLK), f32),
            pltpu.VMEM((NSEQ, 1, BLK), f32),
            pltpu.VMEM((2, 1, 1), f32),
            dma((4,)), dma, dma, dma, dma, dma, dma, dma, dma, dma, dma,
            dma((3,)), dma((3,)), dma((3,)), dma((3,)), dma((3,)),
            dma((3,)), dma((3,)), dma, dma((3,)), dma((3,)),
            dma, dma, dma((8,)), dma, dma, dma,
        ],
        compiler_params=pltpu.CompilerParams(
            collective_id=0, has_side_effects=True, vmem_limit_bytes=56 * 1024 * 1024
        ),
        name="guided_block",
    )(
        lengths, timesteps, labels,
        patches_t, time_w1, time_w2, label_table, jnp.transpose(mod_w), jnp.asarray(rates), qkv_w, jnp.transpose(out_w),
        jnp.transpose(head_w), patch_w, *position_factors(),
    )
    guided, norms, top = pl.pallas_call(
        finish,
        out_shape=(
            jax.ShapeDtypeStruct((NREQ, 8, SLOT), f32),
            jax.ShapeDtypeStruct((1, NREQ), f32),
            jax.ShapeDtypeStruct((NREQ, HEADS), f32),
        ),
        in_specs=[smem] * 2 + [vmem] * 4,
        out_specs=(vmem, vmem, vmem),
        name="guided_finish",
    )(lengths, timesteps, patches_t, noise_t, pred, stats)
    return (jnp.transpose(guided, (0, 2, 1)), norms, top[None, :, :])


def solution(mesh):
    in_specs = (
        P("req", "seq", None),
        P("req", "seq", None),
        P(), P(), P(), P(), P(), P(), P(),
        P(None, ("req", "seq")),
        P("req", None),
        P(None, "req"),
        P(),
    )
    out_specs = (P("req", "seq", "cfg"), P("cfg", "req"), P("cfg", "req", None))
    return jax.shard_map(body, mesh=mesh, in_specs=in_specs, out_specs=out_specs, check_vma=False)
```
